32 devices in a mesh: video: 4 (over x, core), frame: 8 (over z, y).
Axes of the slice: x: 2, y: 2, z: 4, core: 2. Of those that a mesh axis runs over, the one named last changes fastest.
Arguments:
- frames: bfloat16 [32, 1024, 640], P(('video', 'frame')), parts along dimension 0, may hold values from -6 to 6
- ref_rows: bfloat16 [4096, 640], P(('video', 'frame')), parts along dimension 0, may hold values from -6 to 6
- w_query: bfloat16 [640, 640], replicated, may hold values from -1 to 1
- w_key: bfloat16 [640, 640], replicated, may hold values from -1 to 1
- w_value: bfloat16 [640, 640], replicated, may hold values from -0.25 to 0.25
- w_out: bfloat16 [640, 640], replicated, may hold values from -0.25 to 0.25
- w_conv: bfloat16 [3, 640, 640], replicated, may hold values from -0.125 to 0.125
- t_query: bfloat16 [640, 640], replicated, may hold values from -1 to 1
- t_key: bfloat16 [640, 640], replicated, may hold values from -1 to 1
- t_value: bfloat16 [640, 640], replicated, may hold values from -0.25 to 0.25
- t_out: bfloat16 [640, 640], replicated, may hold values from -0.25 to 0.25
Outputs:
- result: bfloat16 [32, 1024, 640], P(('video', 'frame')), parts along dimension 0
The draws below stay inside these ranges and needn't reach their ends.
There are 4 independent parts, one for each index of `video`. The reference program is written for one: setup_inputs(seed, part) draws one part's arguments, and reference() takes and returns one part's arrays. A program takes and returns all parts, laid end to end along the dimension named above; an argument that names none is the same for every part. Nothing has to cross between parts.
All inputs are finite; a program needn't handle non-finite values.
Results may differ from the reference program's by a relative error of at most 0.011.
Values may be sent and summed in bfloat16 or wider, within the bound.
A program may use at most 128 MiB of HBM per device.

```python
import math
import jax
import jax.numpy as jnp
from jax import lax

C = 640
HEADS = 10
HW = 1024
FRAMES = 8


def own_part(key, tag):
    return jax.random.normal(jax.random.fold_in(key, tag), (C, C), jnp.float32)


def draw_w_query(key, part):
    value = own_part(key, 21) / math.sqrt(C)
    return jnp.clip(value, -1.0, 1.0).astype(jnp.bfloat16)


def draw_w_key(key, part):
    value = own_part(key, 22) / math.sqrt(C)
    return jnp.clip(value, -1.0, 1.0).astype(jnp.bfloat16)


def draw_t_query(key, part):
    value = own_part(key, 23) / math.sqrt(C)
    return jnp.clip(value, -1.0, 1.0).astype(jnp.bfloat16)


def draw_t_key(key, part):
    value = own_part(key, 24) / math.sqrt(C)
    return jnp.clip(value, -1.0, 1.0).astype(jnp.bfloat16)


def shard_levels(stream_key, extent, shards, least, largest):
    factor_of, own = 1.0, jax.random.fold_in(stream_key, 6)
    for axis_at, blocks in shards:
        heights = jnp.exp(jax.random.uniform(jax.random.fold_in(own, axis_at), (blocks,), jnp.float32, least / len(shards), largest / len(shards)))
        factor_of = factor_of * jnp.repeat(heights, extent[axis_at] // blocks).reshape([-1 if axis == axis_at else 1 for axis in range(len(extent))])
    return factor_of


def centred(key, shape, scale, reach, pieces=(), dtype=jnp.bfloat16):
    entries = jax.random.normal(key, shape, jnp.float32) * scale
    if len(pieces) > 0:
        entries = shard_levels(key, shape, pieces, -0.22, 0.18) * entries
    return jnp.clip(entries, min=-reach, max=reach).astype(dtype)


def setup_inputs(seed: int = 0, part: int = 0) -> dict:
    arg_keys = jax.random.split(jax.random.key(seed), 12)
    part_splits = jax.random.split(jax.random.fold_in(arg_keys[11], part), 12)
    frames = centred(part_splits[0], (FRAMES, HW, C), 1.0, 6.0, ((0, 8),))
    ref_rows = centred(part_splits[1], (HW, C), 1.0, 6.0, ((0, 8),))
    w_query = draw_w_query(jax.random.fold_in(arg_keys[11], 71), part)
    w_key = draw_w_key(jax.random.fold_in(arg_keys[11], 71), part)
    w_value = centred(arg_keys[4], (C, C), C ** -0.5, 0.25)
    w_out = centred(arg_keys[5], (C, C), C ** -0.5, 0.25)
    w_conv = centred(arg_keys[6], (3, C, C), (3 * C) ** -0.5, 0.125)
    t_query = draw_t_query(jax.random.fold_in(arg_keys[11], 71), part)
    t_key = draw_t_key(jax.random.fold_in(arg_keys[11], 71), part)
    t_value = centred(arg_keys[9], (C, C), C ** -0.5, 0.25)
    t_out = centred(arg_keys[10], (C, C), C ** -0.5, 0.25)
    return dict(frames=frames, ref_rows=ref_rows, w_query=w_query, w_key=w_key, w_value=w_value, w_out=w_out, w_conv=w_conv, t_query=t_query, t_key=t_key, t_value=t_value, t_out=t_out)


def rounded(value):
    return lax.optimization_barrier(value.astype(jnp.bfloat16)).astype(jnp.float32)

def layer_norm(value):
    mean = lax.optimization_barrier(jnp.mean(value, axis=-1, keepdims=True))
    centered = value - mean
    var = lax.optimization_barrier(jnp.mean(centered * centered, axis=-1, keepdims=True))
    return centered * lax.rsqrt(var + 1e-05)

def project(rows, weight):
    return jnp.dot(rows, weight, preferred_element_type=jnp.float32).astype(jnp.bfloat16)

def reference(frames, ref_rows, w_query, w_key, w_value, w_out, w_conv, t_query, t_key, t_value, t_out):
    nframes, pixels, width = frames.shape
    head_dim = width // HEADS
    scale = 1.0 / math.sqrt(head_dim)
    normed = layer_norm(frames.astype(jnp.float32)).astype(jnp.bfloat16).reshape(-1, width)
    query = project(normed, w_query).astype(jnp.float32).reshape(nframes, pixels, HEADS, head_dim)
    keys = project(normed, w_key).astype(jnp.float32).reshape(nframes, pixels, HEADS, head_dim)
    values = project(normed, w_value).astype(jnp.float32).reshape(nframes, pixels, HEADS, head_dim)
    ref_keys = project(ref_rows, w_key).astype(jnp.float32).reshape(pixels, HEADS, head_dim)
    ref_values = project(ref_rows, w_value).astype(jnp.float32).reshape(pixels, HEADS, head_dim)

    def one_head(args):
        qa, ka, va, rka, rva = args
        own = jnp.einsum('fqd,fkd->fqk', qa, ka) * scale
        far = jnp.einsum('fqd,kd->fqk', qa, rka) * scale
        scores = jnp.concatenate([own, far], axis=-1)
        peak = lax.optimization_barrier(jnp.max(scores, axis=-1, keepdims=True))
        expo = jnp.exp(scores - peak)
        total = lax.optimization_barrier(jnp.sum(expo, axis=-1))
        weights = rounded(expo)
        mixed = jnp.einsum('fqk,fkd->fqd', weights[:, :, :pixels], va)
        mixed = mixed + jnp.einsum('fqk,kd->fqd', weights[:, :, pixels:], rva)
        return mixed / total[..., None]
    per_head = lax.map(one_head, (query.transpose(2, 0, 1, 3), keys.transpose(2, 0, 1, 3), values.transpose(2, 0, 1, 3), ref_keys.transpose(1, 0, 2), ref_values.transpose(1, 0, 2)))
    attended = per_head.transpose(1, 2, 0, 3).reshape(-1, width).astype(jnp.bfloat16)
    first = (frames.astype(jnp.float32) + jnp.dot(attended, w_out, preferred_element_type=jnp.float32).reshape(nframes, pixels, width)).astype(jnp.bfloat16)
    padded = jnp.pad(first, ((1, 1), (0, 0), (0, 0)))
    conv = jnp.zeros((nframes * pixels, width), jnp.float32)
    for tap in range(3):
        conv = conv + jnp.dot(padded[tap:tap + nframes].reshape(-1, width), w_conv[tap], preferred_element_type=jnp.float32)
    second = (first.astype(jnp.float32) + conv.reshape(nframes, pixels, width)).astype(jnp.bfloat16)
    normed2 = layer_norm(second.astype(jnp.float32)).astype(jnp.bfloat16).reshape(-1, width)
    tquery = project(normed2, t_query).astype(jnp.float32).reshape(nframes, pixels, HEADS, head_dim)
    tkeys = project(normed2, t_key).astype(jnp.float32).reshape(nframes, pixels, HEADS, head_dim)
    tvalues = project(normed2, t_value).astype(jnp.float32).reshape(nframes, pixels, HEADS, head_dim)
    tscores = jnp.einsum('fnhd,gnhd->nhfg', tquery, tkeys) * scale
    tpeak = lax.optimization_barrier(jnp.max(tscores, axis=-1, keepdims=True))
    texpo = jnp.exp(tscores - tpeak)
    ttotal = lax.optimization_barrier(jnp.sum(texpo, axis=-1))
    tmixed = jnp.einsum('nhfg,gnhd->nhfd', rounded(texpo), tvalues) / ttotal[..., None]
    tattended = tmixed.transpose(2, 0, 1, 3).reshape(-1, width).astype(jnp.bfloat16)
    result = second.astype(jnp.float32) + jnp.dot(tattended, t_out, preferred_element_type=jnp.float32).reshape(nframes, pixels, width)
    return result.astype(jnp.bfloat16)
```

```python
import functools
import math

import jax
import jax.numpy as jnp
from jax import lax
from jax.experimental import pallas as pl
from jax.experimental.pallas import tpu as pltpu
from jax.sharding import PartitionSpec as P

HEADS = 10
F32 = jnp.float32
BF16 = jnp.bfloat16
LOG2E = math.log2(math.e)
CHUNKS = 2


def layer_norm(value):
    mean = jnp.mean(value, axis=-1, keepdims=True)
    centered = value - mean
    var = jnp.mean(centered * centered, axis=-1, keepdims=True)
    return centered * lax.rsqrt(var + 1e-05)


def dot(a, b):
    return jnp.dot(a, b, preferred_element_type=F32)


def dot_nt(a, b):
    return lax.dot_general(a, b, (((1,), (1,)), ((), ())), preferred_element_type=F32)


def remote(src, dst, send, recv, device):
    return pltpu.make_async_remote_copy(
        src_ref=src,
        dst_ref=dst,
        send_sem=send,
        recv_sem=recv,
        device_id={"frame": device},
        device_id_type=pl.DeviceIdType.MESH,
    )


def kernel(
    ndev,
    x_ref,
    own_ref,
    wq,
    wk,
    wv,
    wo,
    wc,
    tq,
    tk,
    tv,
    to,
    out_ref,
    refbuf,
    qbuf,
    kbuf,
    vbuf,
    abuf,
    fbuf,
    rbuf,
    sbuf,
    tqb,
    tkb,
    tvb,
    tab,
    resbuf,
    ref_send,
    ref_recv,
    fwd_send,
    there_send,
    there_recv,
    back_send,
    back_recv,
    local_sem,
):
    pixels, width = x_ref.shape
    pairs = HEADS // 2
    head_dim = width // HEADS
    qscale = LOG2E / math.sqrt(head_dim)
    group = pixels // ndev
    block = 2 * group
    nblocks = pixels // block
    me = lax.axis_index("frame")
    partner = me + 1 - 2 * lax.rem(me, 2)
    line = me // 2

    barrier = pltpu.get_barrier_semaphore()
    for off in range(1, ndev):
        pl.semaphore_signal(
            barrier,
            inc=1,
            device_id={"frame": lax.rem(me + off, ndev)},
            device_id_type=pl.DeviceIdType.MESH,
        )
    pl.semaphore_wait(barrier, ndev - 1)

    def ref_copy(target, slot):
        return remote(own_ref, refbuf.at[me], ref_send.at[slot], ref_recv.at[me], target)

    def ref_forward(owner, slot):
        return remote(
            refbuf.at[owner], refbuf.at[owner], fwd_send.at[slot], ref_recv.at[owner], partner
        )

    hops = ndev // 2
    for hop in range(1, hops):
        ref_copy(lax.rem(me + 2 * hop, ndev), hop).start()
    ref_copy(partner, 0).start()

    def own_rows(step, carry):
        rows = pl.ds(pl.multiple_of(step * block, block), block)
        normed = layer_norm(x_ref[rows, :].astype(F32)).astype(BF16)
        qbuf[rows, :] = (dot(normed, wq[...]) * qscale).astype(BF16)
        kbuf[rows, :] = dot(normed, wk[...]).astype(BF16)
        values = dot(normed, wv[...]).astype(BF16)
        for pair in range(pairs):
            vbuf[pair, rows, 0:128] = values[:, pair * 128 : pair * 128 + 128]
            vbuf[pair, rows, 128:256] = jnp.ones((block, 128), BF16)
        return carry

    lax.fori_loop(0, nblocks, own_rows, 0)

    for hop in range(1, hops):
        owner = lax.rem(me + 2 * hop, ndev)
        ref_forward(owner, hop).wait_recv()
        ref_forward(owner, hop).start()

    def ref_project(rows_in, owner):
        rows = pl.ds(pl.multiple_of(pixels + owner * group, group), group)
        kbuf[rows, :] = dot(rows_in, wk[...]).astype(BF16)
        values = dot(rows_in, wv[...]).astype(BF16)
        for pair in range(pairs):
            vbuf[pair, rows, 0:128] = values[:, pair * 128 : pair * 128 + 128]
            vbuf[pair, rows, 128:256] = jnp.ones((group, 128), BF16)

    ref_project(own_ref[...], me)

    def line_rows(hop, carry):
        owner = lax.rem(me + 2 * hop, ndev)
        ref_project(refbuf[owner], owner)
        return carry

    lax.fori_loop(1, hops, line_rows, 0)

    def partner_rows(hop, carry):
        owner = lax.rem(partner + 2 * hop, ndev)
        ref_forward(owner, 0).wait_recv()
        ref_project(refbuf[owner], owner)
        return carry

    lax.fori_loop(0, hops, partner_rows, 0)

    low = lax.broadcasted_iota(jnp.int32, (block, 128), 1) < 64

    def send_there(target):
        return remote(
            fbuf.at[target], rbuf.at[me], there_send.at[target], there_recv.at[me], target
        )

    def attend(step, carry):
        back = nblocks - 1 - step
        where_to = lax.rem(line + lax.rem((back * (back + 1)) // 2, nblocks), nblocks)
        rows = pl.ds(pl.multiple_of(where_to * block, block), block)

        def one_pair(pair, carry):
            lanes = pl.ds(pl.multiple_of(pair * 128, 128), 128)
            queries = qbuf[rows, lanes]
            keys = kbuf[:, lanes]
            values = vbuf[pair]
            mixed = []
            for half in range(2):
                zero = jnp.zeros_like(queries)
                masked = jnp.where(low, queries, zero) if half == 0 else jnp.where(low, zero, queries)
                scores = dot_nt(masked, keys)
                peak = jnp.max(scores, axis=-1, keepdims=True)
                expo = jnp.exp2(scores - peak).astype(BF16)
                both = dot(expo, values)
                mixed.append(both[:, :128] / both[:, 128:])
            abuf[:, lanes] = jnp.where(low, mixed[0], mixed[1]).astype(BF16)
            return carry

        lax.fori_loop(0, pairs, one_pair, 0)
        first = (x_ref[rows, :].astype(F32) + dot(abuf[...], wo[...])).astype(BF16)
        for half in range(2):
            target = 2 * where_to + half
            fbuf[target] = first[half * group : (half + 1) * group]

            @pl.when(target != me)
            def _():
                send_there(target).start()

        return carry

    lax.fori_loop(0, nblocks, attend, 0)

    keep = pltpu.make_async_copy(fbuf.at[me], rbuf.at[me], local_sem)
    keep.start()
    keep.wait()
    for off in range(1, ndev):
        other = lax.rem(me + off, ndev)
        remote(
            fbuf.at[other], rbuf.at[other], there_send.at[other], there_recv.at[other], other
        ).wait()

    size = group // CHUNKS
    span = ndev * 16
    tlow = lax.broadcasted_iota(jnp.int32, (span, 128), 1) < 64
    same = lax.rem(lax.broadcasted_iota(jnp.int32, (span, span), 0), 16) == lax.rem(
        lax.broadcasted_iota(jnp.int32, (span, span), 1), 16
    )

    def back_copy(chunk, target, sender):
        return remote(
            resbuf.at[chunk, target],
            out_ref.at[pl.ds(pl.multiple_of(sender * group + chunk * size, size), size)],
            back_send.at[chunk * ndev + target],
            back_recv.at[chunk * ndev + sender],
            target,
        )

    def temporal(chunk, carry):
        cols = pl.ds(pl.multiple_of(chunk * size, size), size)
        x = rbuf[:, cols, :].reshape(ndev * size, width)
        edge = jnp.zeros((size, width), BF16)
        before = jnp.concatenate([edge, x[:-size]], axis=0)
        after = jnp.concatenate([x[size:], edge], axis=0)
        conv = dot(before, wc[0]) + dot(x, wc[1]) + dot(after, wc[2])
        second = (x.astype(F32) + conv).astype(BF16)
        sbuf[...] = second
        normed = layer_norm(second.astype(F32)).astype(BF16)
        tqb[...] = (dot(normed, tq[...]) * qscale).astype(BF16).reshape(ndev, size, width)
        tkb[...] = dot(normed, tk[...]).astype(BF16).reshape(ndev, size, width)
        tvb[...] = dot(normed, tv[...]).astype(BF16).reshape(ndev, size, width)

        def sub(index, carry):
            part = pl.ds(pl.multiple_of(index * 16, 16), 16)
            for pair in range(pairs):
                lanes = pl.ds(pair * 128, 128)
                queries = tqb[:, part, lanes].reshape(span, 128)
                keys = tkb[:, part, lanes].reshape(span, 128)
                values = tvb[:, part, lanes].reshape(span, 128)
                zero = jnp.zeros_like(queries)
                mixed = []
                for half in range(2):
                    masked = (
                        jnp.where(tlow, queries, zero) if half == 0 else jnp.where(tlow, zero, queries)
                    )
                    scores = jnp.where(same, dot_nt(masked, keys), -1e30)
                    peak = jnp.max(scores, axis=-1, keepdims=True)
                    expo = jnp.exp2(scores - peak)
                    total = jnp.sum(expo, axis=-1, keepdims=True)
                    mixed.append(dot(expo.astype(BF16), values) / total)
                tab[:, part, lanes] = (
                    jnp.where(tlow, mixed[0], mixed[1]).astype(BF16).reshape(ndev, 16, 128)
                )
            return carry

        lax.fori_loop(0, size // 16, sub, 0)
        result = sbuf[...].astype(F32) + dot(tab[...].reshape(ndev * size, width), to[...])
        resbuf[chunk] = result.astype(BF16).reshape(ndev, size, width)
        for off in range(1, ndev):
            back_copy(chunk, lax.rem(me + off, ndev), me).start()
        out_ref[pl.ds(pl.multiple_of(me * group + chunk * size, size), size), :] = resbuf[chunk, me]
        return carry

    lax.fori_loop(0, CHUNKS, temporal, 0)

    ref_copy(partner, 0).wait_send()
    for hop in range(1, hops):
        owner = lax.rem(me + 2 * hop, ndev)
        ref_copy(owner, hop).wait_send()
        ref_forward(owner, hop).wait_send()
    for chunk in range(CHUNKS):
        for off in range(1, ndev):
            other = lax.rem(me + off, ndev)
            back_copy(chunk, other, me).wait_send()
            back_copy(chunk, other, other).wait_recv()


def per_device(
    frames, ref_rows, w_query, w_key, w_value, w_out, w_conv, t_query, t_key, t_value, t_out
):
    fdev, pixels, width = frames.shape
    ndev = lax.axis_size("frame")
    group = pixels // ndev
    block = 2 * group
    pairs = HEADS // 2
    size = group // CHUNKS
    DMA = pltpu.SemaphoreType.DMA
    out = pl.pallas_call(
        functools.partial(kernel, ndev),
        out_shape=jax.ShapeDtypeStruct((pixels, width), BF16),
        in_specs=[pl.BlockSpec(memory_space=pltpu.VMEM)] * 11,
        out_specs=pl.BlockSpec(memory_space=pltpu.VMEM),
        scratch_shapes=[
            pltpu.VMEM((ndev, group, width), BF16),
            pltpu.VMEM((pixels, width), BF16),
            pltpu.VMEM((2 * pixels, width), BF16),
            pltpu.VMEM((pairs, 2 * pixels, 256), BF16),
            pltpu.VMEM((block, width), BF16),
            pltpu.VMEM((ndev, group, width), BF16),
            pltpu.VMEM((ndev, group, width), BF16),
            pltpu.VMEM((ndev * size, width), BF16),
            pltpu.VMEM((ndev, size, width), BF16),
            pltpu.VMEM((ndev, size, width), BF16),
            pltpu.VMEM((ndev, size, width), BF16),
            pltpu.VMEM((ndev, size, width), BF16),
            pltpu.VMEM((CHUNKS, ndev, size, width), BF16),
            DMA((ndev,)),
            DMA((ndev,)),
            DMA((ndev,)),
            DMA((ndev,)),
            DMA((ndev,)),
            DMA((CHUNKS * ndev,)),
            DMA((CHUNKS * ndev,)),
            DMA(()),
        ],
        compiler_params=pltpu.CompilerParams(
            collective_id=0, has_side_effects=True, vmem_limit_bytes=60 * 1024 * 1024
        ),
    )(
        frames.reshape(pixels, width),
        ref_rows,
        w_query,
        w_key,
        w_value,
        w_out,
        w_conv,
        t_query,
        t_key,
        t_value,
        t_out,
    )
    return out.reshape(fdev, pixels, width)


def solution(mesh):
    return jax.shard_map(
        per_device,
        mesh=mesh,
        in_specs=(
            P(("video", "frame"), None, None),
            P(("video", "frame"), None),
            P(),
            P(),
            P(),
            P(),
            P(),
            P(),
            P(),
            P(),
            P(),
        ),
        out_specs=P(("video", "frame"), None, None),
        check_vma=False,
    )
```

```python
import functools
import math

import jax
import jax.numpy as jnp
from jax import lax
from jax.experimental import pallas as pl
from jax.experimental.pallas import tpu as pltpu
from jax.sharding import PartitionSpec as P

HEADS = 10
F32 = jnp.float32
BF16 = jnp.bfloat16
LOG2E = math.log2(math.e)
CHUNKS = 4


def layer_norm(value):
    mean = jnp.mean(value, axis=-1, keepdims=True)
    centered = value - mean
    var = jnp.mean(centered * centered, axis=-1, keepdims=True)
    return centered * lax.rsqrt(var + 1e-05)


def dot(a, b):
    return jnp.dot(a, b, preferred_element_type=F32)


def dot_nt(a, b):
    return lax.dot_general(a, b, (((1,), (1,)), ((), ())), preferred_element_type=F32)


def remote(src, dst, send, recv, device):
    return pltpu.make_async_remote_copy(
        src_ref=src,
        dst_ref=dst,
        send_sem=send,
        recv_sem=recv,
        device_id={"frame": device},
        device_id_type=pl.DeviceIdType.MESH,
    )


def kernel(
    ndev,
    x_ref,
    own_ref,
    wq,
    wk,
    wv,
    wo,
    wc,
    tq,
    tk,
    tv,
    to,
    out_ref,
    refbuf,
    qbuf,
    kbuf,
    vbuf,
    abuf,
    fbuf,
    rbuf,
    sbuf,
    tqb,
    tkb,
    tvb,
    tab,
    resbuf,
    ref_send,
    ref_recv,
    fwd_send,
    there_send,
    there_recv,
    back_send,
    back_recv,
):
    group, width = x_ref.shape[1:]
    pixels = ndev * group
    pairs = HEADS // 2
    head_dim = width // HEADS
    qscale = LOG2E / math.sqrt(head_dim)
    size = group // CHUNKS
    block = ndev * size
    me = lax.axis_index("frame")
    partner = me + 1 - 2 * lax.rem(me, 2)

    barrier = pltpu.get_barrier_semaphore()
    for off in range(1, ndev):
        pl.semaphore_signal(
            barrier,
            inc=1,
            device_id={"frame": lax.rem(me + off, ndev)},
            device_id_type=pl.DeviceIdType.MESH,
        )
    pl.semaphore_wait(barrier, ndev - 1)

    def ref_copy(target, slot):
        return remote(own_ref, refbuf.at[me], ref_send.at[slot], ref_recv.at[me], target)

    def ref_forward(owner, slot):
        return remote(
            refbuf.at[owner], refbuf.at[owner], fwd_send.at[slot], ref_recv.at[owner], partner
        )

    hops = ndev // 2
    for hop in range(1, hops):
        ref_copy(lax.rem(me + 2 * hop, ndev), hop).start()
    ref_copy(partner, 0).start()

    def own_rows(step, carry):
        rows = pl.ds(pl.multiple_of(step * 2 * group, 2 * group), 2 * group)
        both = pl.ds(step * 2, 2)
        x = x_ref[both].reshape(2 * group, width)
        normed = layer_norm(x.astype(F32)).astype(BF16)
        queries = (dot(normed, wq[...]) * qscale).astype(BF16)
        qbuf[both] = queries.reshape(2, group, width)
        kbuf[rows, :] = dot(normed, wk[...]).astype(BF16)
        values = dot(normed, wv[...]).astype(BF16)
        for pair in range(pairs):
            vbuf[pair, rows, 0:128] = values[:, pair * 128 : pair * 128 + 128]
            vbuf[pair, rows, 128:256] = jnp.ones((2 * group, 128), BF16)
        return carry

    lax.fori_loop(0, ndev // 2, own_rows, 0)

    for hop in range(1, hops):
        owner = lax.rem(me + 2 * hop, ndev)
        ref_forward(owner, hop).wait_recv()
        ref_forward(owner, hop).start()

    def ref_project(rows_in, owner):
        rows = pl.ds(pl.multiple_of(pixels + owner * group, group), group)
        kbuf[rows, :] = dot(rows_in, wk[...]).astype(BF16)
        values = dot(rows_in, wv[...]).astype(BF16)
        for pair in range(pairs):
            vbuf[pair, rows, 0:128] = values[:, pair * 128 : pair * 128 + 128]
            vbuf[pair, rows, 128:256] = jnp.ones((group, 128), BF16)

    ref_project(own_ref[...], me)

    def line_rows(hop, carry):
        owner = lax.rem(me + 2 * hop, ndev)
        ref_project(refbuf[owner], owner)
        return carry

    lax.fori_loop(1, hops, line_rows, 0)

    def partner_rows(hop, carry):
        owner = lax.rem(partner + 2 * hop, ndev)
        ref_forward(owner, 0).wait_recv()
        ref_project(refbuf[owner], owner)
        return carry

    lax.fori_loop(0, hops, partner_rows, 0)

    low = lax.broadcasted_iota(jnp.int32, (block, 128), 1) < 64

    def there_copy(chunk, target, sender):
        return remote(
            fbuf.at[chunk, target],
            rbuf.at[chunk, sender],
            there_send.at[chunk * ndev + target],
            there_recv.at[chunk * ndev + sender],
            target,
        )

    def attend(chunk):
        rows = pl.ds(pl.multiple_of(chunk * size, size), size)

        for pair in range(pairs):
            lanes = pl.ds(pair * 128, 128)
            queries = qbuf[:, rows, lanes].reshape(block, 128)
            keys = kbuf[:, lanes]
            values = vbuf[pair]
            mixed = []
            for half in range(2):
                zero = jnp.zeros_like(queries)
                masked = jnp.where(low, queries, zero) if half == 0 else jnp.where(low, zero, queries)
                scores = dot_nt(masked, keys)
                peak = jnp.max(scores, axis=-1, keepdims=True)
                expo = jnp.exp2(scores - peak).astype(BF16)
                both = dot(expo, values)
                mixed.append(both[:, :128] / both[:, 128:])
            abuf[:, lanes] = jnp.where(low, mixed[0], mixed[1]).astype(BF16)

        x = x_ref[:, rows, :].reshape(block, width).astype(F32)
        first = (x + dot(abuf[...], wo[...])).astype(BF16)
        fbuf[chunk] = first.reshape(ndev, size, width)
        for off in reversed(range(1, ndev)):
            there_copy(chunk, lax.rem(me + off, ndev), me).start()
        rbuf[chunk, me] = fbuf[chunk, me]

    span = ndev * 16
    tlow = lax.broadcasted_iota(jnp.int32, (span, 128), 1) < 64
    same = lax.rem(lax.broadcasted_iota(jnp.int32, (span, span), 0), 16) == lax.rem(
        lax.broadcasted_iota(jnp.int32, (span, span), 1), 16
    )

    def back_copy(chunk, target, sender):
        return remote(
            resbuf.at[chunk, target],
            out_ref.at[pl.ds(pl.multiple_of(sender * group + chunk * size, size), size)],
            back_send.at[chunk * ndev + target],
            back_recv.at[chunk * ndev + sender],
            target,
        )

    def temporal(chunk):
        for off in range(1, ndev):
            there_copy(chunk, lax.rem(me + off, ndev), lax.rem(me + off, ndev)).wait_recv()
        x = rbuf[chunk].reshape(ndev * size, width)
        edge = jnp.zeros((size, width), BF16)
        before = jnp.concatenate([edge, x[:-size]], axis=0)
        after = jnp.concatenate([x[size:], edge], axis=0)
        conv = dot(before, wc[0]) + dot(x, wc[1]) + dot(after, wc[2])
        second = (x.astype(F32) + conv).astype(BF16)
        sbuf[...] = second
        normed = layer_norm(second.astype(F32)).astype(BF16)
        tqb[...] = (dot(normed, tq[...]) * qscale).astype(BF16).reshape(ndev, size, width)
        tkb[...] = dot(normed, tk[...]).astype(BF16).reshape(ndev, size, width)
        tvb[...] = dot(normed, tv[...]).astype(BF16).reshape(ndev, size, width)

        def sub(index, carry):
            part = pl.ds(pl.multiple_of(index * 16, 16), 16)
            for pair in range(pairs):
                lanes = pl.ds(pair * 128, 128)
                queries = tqb[:, part, lanes].reshape(span, 128)
                keys = tkb[:, part, lanes].reshape(span, 128)
                values = tvb[:, part, lanes].reshape(span, 128)
                zero = jnp.zeros_like(queries)
                mixed = []
                for half in range(2):
                    masked = (
                        jnp.where(tlow, queries, zero) if half == 0 else jnp.where(tlow, zero, queries)
                    )
                    scores = jnp.where(same, dot_nt(masked, keys), -1e30)
                    peak = jnp.max(scores, axis=-1, keepdims=True)
                    expo = jnp.exp2(scores - peak)
                    total = jnp.sum(expo, axis=-1, keepdims=True)
                    mixed.append(dot(expo.astype(BF16), values) / total)
                tab[:, part, lanes] = (
                    jnp.where(tlow, mixed[0], mixed[1]).astype(BF16).reshape(ndev, 16, 128)
                )
            return carry

        lax.fori_loop(0, size // 16, sub, 0)
        result = sbuf[...].astype(F32) + dot(tab[...].reshape(ndev * size, width), to[...])
        resbuf[chunk] = result.astype(BF16).reshape(ndev, size, width)
        for off in range(1, ndev):
            back_copy(chunk, lax.rem(me + off, ndev), me).start()
        out_ref[pl.ds(pl.multiple_of(me * group + chunk * size, size), size), :] = resbuf[chunk, me]

    def stage(step, carry):
        @pl.when(step < CHUNKS)
        def _():
            attend(step)

        @pl.when(step >= 1)
        def _():
            temporal(step - 1)

        return carry

    lax.fori_loop(0, CHUNKS + 1, stage, 0)

    ref_copy(partner, 0).wait_send()
    for hop in range(1, hops):
        owner = lax.rem(me + 2 * hop, ndev)
        ref_copy(owner, hop).wait_send()
        ref_forward(owner, hop).wait_send()
    for chunk in range(CHUNKS):
        for off in range(1, ndev):
            other = lax.rem(me + off, ndev)
            there_copy(chunk, other, me).wait_send()
            back_copy(chunk, other, me).wait_send()
            back_copy(chunk, other, other).wait_recv()


def per_device(
    frames, ref_rows, w_query, w_key, w_value, w_out, w_conv, t_query, t_key, t_value, t_out
):
    fdev, pixels, width = frames.shape
    ndev = lax.axis_size("frame")
    group = pixels // ndev
    pairs = HEADS // 2
    size = group // CHUNKS
    block = ndev * size
    DMA = pltpu.SemaphoreType.DMA
    out = pl.pallas_call(
        functools.partial(kernel, ndev),
        out_shape=jax.ShapeDtypeStruct((pixels, width), BF16),
        in_specs=[pl.BlockSpec(memory_space=pltpu.VMEM)] * 11,
        out_specs=pl.BlockSpec(memory_space=pltpu.VMEM),
        scratch_shapes=[
            pltpu.VMEM((ndev, group, width), BF16),
            pltpu.VMEM((ndev, group, width), BF16),
            pltpu.VMEM((2 * pixels, width), BF16),
            pltpu.VMEM((pairs, 2 * pixels, 256), BF16),
            pltpu.VMEM((block, width), BF16),
            pltpu.VMEM((CHUNKS, ndev, size, width), BF16),
            pltpu.VMEM((CHUNKS, ndev, size, width), BF16),
            pltpu.VMEM((block, width), BF16),
            pltpu.VMEM((ndev, size, width), BF16),
            pltpu.VMEM((ndev, size, width), BF16),
            pltpu.VMEM((ndev, size, width), BF16),
            pltpu.VMEM((ndev, size, width), BF16),
            pltpu.VMEM((CHUNKS, ndev, size, width), BF16),
            DMA((ndev,)),
            DMA((ndev,)),
            DMA((ndev,)),
            DMA((CHUNKS * ndev,)),
            DMA((CHUNKS * ndev,)),
            DMA((CHUNKS * ndev,)),
            DMA((CHUNKS * ndev,)),
        ],
        compiler_params=pltpu.CompilerParams(
            collective_id=0, has_side_effects=True, vmem_limit_bytes=60 * 1024 * 1024
        ),
    )(
        frames.reshape(ndev, group, width),
        ref_rows,
        w_query,
        w_key,
        w_value,
        w_out,
        w_conv,
        t_query,
        t_key,
        t_value,
        t_out,
    )
    return out.reshape(fdev, pixels, width)


def solution(mesh):
    return jax.shard_map(
        per_device,
        mesh=mesh,
        in_specs=(
            P(("video", "frame"), None, None),
            P(("video", "frame"), None),
            P(),
            P(),
            P(),
            P(),
            P(),
            P(),
            P(),
            P(),
            P(),
        ),
        out_specs=P(("video", "frame"), None, None),
        check_vma=False,
    )
```

```python
import functools
import math

import jax
import jax.numpy as jnp
from jax import lax
from jax.experimental import pallas as pl
from jax.experimental.pallas import tpu as pltpu
from jax.sharding import PartitionSpec as P

HEADS = 10
F32 = jnp.float32
BF16 = jnp.bfloat16
LOG2E = math.log2(math.e)
CHUNKS = 4


def layer_norm(value):
    mean = jnp.mean(value, axis=-1, keepdims=True)
    centered = value - mean
    var = jnp.mean(centered * centered, axis=-1, keepdims=True)
    return centered * lax.rsqrt(var + 1e-05)


def dot(a, b):
    return jnp.dot(a, b, preferred_element_type=F32)


def dot_nt(a, b):
    return lax.dot_general(a, b, (((1,), (1,)), ((), ())), preferred_element_type=F32)


def remote(src, dst, send, recv, device):
    return pltpu.make_async_remote_copy(
        src_ref=src,
        dst_ref=dst,
        send_sem=send,
        recv_sem=recv,
        device_id={"frame": device},
        device_id_type=pl.DeviceIdType.MESH,
    )


def kernel(
    ndev,
    x_ref,
    own_ref,
    wq,
    wk,
    wv,
    wo,
    wc,
    tq,
    tk,
    tv,
    to,
    out_ref,
    refbuf,
    qbuf,
    kbuf,
    vbuf,
    abuf,
    fbuf,
    rbuf,
    sbuf,
    tqb,
    tkb,
    tvb,
    tab,
    resbuf,
    ref_send,
    ref_recv,
    fwd_send,
    there_send,
    there_recv,
    back_send,
    back_recv,
):
    group, width = x_ref.shape[1:]
    pixels = ndev * group
    pairs = HEADS // 2
    head_dim = width // HEADS
    qscale = LOG2E / math.sqrt(head_dim)
    size = group // CHUNKS
    block = ndev * size
    me = lax.axis_index("frame")
    partner = me + 1 - 2 * lax.rem(me, 2)

    barrier = pltpu.get_barrier_semaphore()
    for off in range(1, ndev):
        pl.semaphore_signal(
            barrier,
            inc=1,
            device_id={"frame": lax.rem(me + off, ndev)},
            device_id_type=pl.DeviceIdType.MESH,
        )
    pl.semaphore_wait(barrier, ndev - 1)

    def ref_copy(target, slot):
        return remote(own_ref, refbuf.at[me], ref_send.at[slot], ref_recv.at[me], target)

    def ref_forward(owner, slot):
        return remote(
            refbuf.at[owner], refbuf.at[owner], fwd_send.at[slot], ref_recv.at[owner], partner
        )

    hops = ndev // 2
    for hop in range(1, hops):
        ref_copy(lax.rem(me + 2 * hop, ndev), hop).start()
    ref_copy(partner, 0).start()

    def own_rows(step, carry):
        rows = pl.ds(pl.multiple_of(step * 2 * group, 2 * group), 2 * group)
        both = pl.ds(step * 2, 2)
        x = x_ref[both].reshape(2 * group, width)
        normed = layer_norm(x.astype(F32)).astype(BF16)
        queries = (dot(normed, wq[...]) * qscale).astype(BF16)
        qbuf[both] = queries.reshape(2, group, width)
        kbuf[rows, :] = dot(normed, wk[...]).astype(BF16)
        values = dot(normed, wv[...]).astype(BF16)
        for pair in range(pairs):
            vbuf[pair, rows, 0:128] = values[:, pair * 128 : pair * 128 + 128]
            vbuf[pair, rows, 128:256] = jnp.ones((2 * group, 128), BF16)
        return carry

    lax.fori_loop(0, ndev // 2, own_rows, 0)

    for hop in range(1, hops):
        owner = lax.rem(me + 2 * hop, ndev)
        ref_forward(owner, hop).wait_recv()
        ref_forward(owner, hop).start()

    def ref_project(rows_in, owner):
        rows = pl.ds(pl.multiple_of(pixels + owner * group, group), group)
        kbuf[rows, :] = dot(rows_in, wk[...]).astype(BF16)
        values = dot(rows_in, wv[...]).astype(BF16)
        for pair in range(pairs):
            vbuf[pair, rows, 0:128] = values[:, pair * 128 : pair * 128 + 128]
            vbuf[pair, rows, 128:256] = jnp.ones((group, 128), BF16)

    ref_project(own_ref[...], me)

    def line_rows(hop, carry):
        owner = lax.rem(me + 2 * hop, ndev)
        ref_project(refbuf[owner], owner)
        return carry

    lax.fori_loop(1, hops, line_rows, 0)

    def partner_rows(hop, carry):
        owner = lax.rem(partner + 2 * hop, ndev)
        ref_forward(owner, 0).wait_recv()
        ref_project(refbuf[owner], owner)
        return carry

    lax.fori_loop(0, hops, partner_rows, 0)

    low = lax.broadcasted_iota(jnp.int32, (block, 128), 1) < 64

    def there_copy(chunk, target, sender):
        return remote(
            fbuf.at[chunk, target],
            rbuf.at[chunk, sender],
            there_send.at[chunk * ndev + target],
            there_recv.at[chunk * ndev + sender],
            target,
        )

    def attend(chunk):
        rows = pl.ds(pl.multiple_of(chunk * size, size), size)

        for pair in range(pairs):
            lanes = pl.ds(pair * 128, 128)
            queries = qbuf[:, rows, lanes].reshape(block, 128)
            keys = kbuf[:, lanes]
            values = vbuf[pair]
            mixed = []
            for half in range(2):
                zero = jnp.zeros_like(queries)
                masked = jnp.where(low, queries, zero) if half == 0 else jnp.where(low, zero, queries)
                scores = dot_nt(masked, keys)
                peak = jnp.max(scores, axis=-1, keepdims=True)
                expo = jnp.exp2((scores - peak).astype(BF16))
                both = dot(expo, values)
                mixed.append(both[:, :128] / both[:, 128:])
            abuf[:, lanes] = jnp.where(low, mixed[0], mixed[1]).astype(BF16)

        x = x_ref[:, rows, :].reshape(block, width).astype(F32)
        first = (x + dot(abuf[...], wo[...])).astype(BF16)
        fbuf[chunk] = first.reshape(ndev, size, width)
        for off in reversed(range(1, ndev)):
            there_copy(chunk, lax.rem(me + off, ndev), me).start()
        rbuf[chunk, me] = fbuf[chunk, me]

    span = ndev * 16
    tlow = lax.broadcasted_iota(jnp.int32, (span, 128), 1) < 64
    same = lax.rem(lax.broadcasted_iota(jnp.int32, (span, span), 0), 16) == lax.rem(
        lax.broadcasted_iota(jnp.int32, (span, span), 1), 16
    )

    def back_copy(chunk, target, sender):
        return remote(
            resbuf.at[chunk, target],
            out_ref.at[pl.ds(pl.multiple_of(sender * group + chunk * size, size), size)],
            back_send.at[chunk * ndev + target],
            back_recv.at[chunk * ndev + sender],
            target,
        )

    def temporal(chunk):
        for off in range(1, ndev):
            there_copy(chunk, lax.rem(me + off, ndev), lax.rem(me + off, ndev)).wait_recv()
        x = rbuf[chunk].reshape(ndev * size, width)
        edge = jnp.zeros((size, width), BF16)
        before = jnp.concatenate([edge, x[:-size]], axis=0)
        after = jnp.concatenate([x[size:], edge], axis=0)
        conv = dot(before, wc[0]) + dot(x, wc[1]) + dot(after, wc[2])
        second = (x.astype(F32) + conv).astype(BF16)
        sbuf[...] = second
        normed = layer_norm(second.astype(F32)).astype(BF16)
        tqb[...] = (dot(normed, tq[...]) * qscale).astype(BF16).reshape(ndev, size, width)
        tkb[...] = dot(normed, tk[...]).astype(BF16).reshape(ndev, size, width)
        tvb[...] = dot(normed, tv[...]).astype(BF16).reshape(ndev, size, width)

        def sub(index, carry):
            part = pl.ds(pl.multiple_of(index * 16, 16), 16)
            for pair in range(pairs):
                lanes = pl.ds(pair * 128, 128)
                queries = tqb[:, part, lanes].reshape(span, 128)
                keys = tkb[:, part, lanes].reshape(span, 128)
                values = tvb[:, part, lanes].reshape(span, 128)
                zero = jnp.zeros_like(queries)
                mixed = []
                for half in range(2):
                    masked = (
                        jnp.where(tlow, queries, zero) if half == 0 else jnp.where(tlow, zero, queries)
                    )
                    scores = jnp.where(same, dot_nt(masked, keys), -1e30)
                    peak = jnp.max(scores, axis=-1, keepdims=True)
                    expo = jnp.exp2(scores - peak)
                    total = jnp.sum(expo, axis=-1, keepdims=True)
                    mixed.append(dot(expo.astype(BF16), values) / total)
                tab[:, part, lanes] = (
                    jnp.where(tlow, mixed[0], mixed[1]).astype(BF16).reshape(ndev, 16, 128)
                )
            return carry

        lax.fori_loop(0, size // 16, sub, 0)
        result = sbuf[...].astype(F32) + dot(tab[...].reshape(ndev * size, width), to[...])
        resbuf[chunk] = result.astype(BF16).reshape(ndev, size, width)
        for off in range(1, ndev):
            back_copy(chunk, lax.rem(me + off, ndev), me).start()
        out_ref[pl.ds(pl.multiple_of(me * group + chunk * size, size), size), :] = resbuf[chunk, me]

    def stage(step, carry):
        @pl.when(step < CHUNKS)
        def _():
            attend(step)

        @pl.when(step >= 1)
        def _():
            temporal(step - 1)

        return carry

    lax.fori_loop(0, CHUNKS + 1, stage, 0)

    ref_copy(partner, 0).wait_send()
    for hop in range(1, hops):
        owner = lax.rem(me + 2 * hop, ndev)
        ref_copy(owner, hop).wait_send()
        ref_forward(owner, hop).wait_send()
    for chunk in range(CHUNKS):
        for off in range(1, ndev):
            other = lax.rem(me + off, ndev)
            there_copy(chunk, other, me).wait_send()
            back_copy(chunk, other, me).wait_send()
            back_copy(chunk, other, other).wait_recv()


def per_device(
    frames, ref_rows, w_query, w_key, w_value, w_out, w_conv, t_query, t_key, t_value, t_out
):
    fdev, pixels, width = frames.shape
    ndev = lax.axis_size("frame")
    group = pixels // ndev
    pairs = HEADS // 2
    size = group // CHUNKS
    block = ndev * size
    DMA = pltpu.SemaphoreType.DMA
    out = pl.pallas_call(
        functools.partial(kernel, ndev),
        out_shape=jax.ShapeDtypeStruct((pixels, width), BF16),
        in_specs=[pl.BlockSpec(memory_space=pltpu.VMEM)] * 11,
        out_specs=pl.BlockSpec(memory_space=pltpu.VMEM),
        scratch_shapes=[
            pltpu.VMEM((ndev, group, width), BF16),
            pltpu.VMEM((ndev, group, width), BF16),
            pltpu.VMEM((2 * pixels, width), BF16),
            pltpu.VMEM((pairs, 2 * pixels, 256), BF16),
            pltpu.VMEM((block, width), BF16),
            pltpu.VMEM((CHUNKS, ndev, size, width), BF16),
            pltpu.VMEM((CHUNKS, ndev, size, width), BF16),
            pltpu.VMEM((block, width), BF16),
            pltpu.VMEM((ndev, size, width), BF16),
            pltpu.VMEM((ndev, size, width), BF16),
            pltpu.VMEM((ndev, size, width), BF16),
            pltpu.VMEM((ndev, size, width), BF16),
            pltpu.VMEM((CHUNKS, ndev, size, width), BF16),
            DMA((ndev,)),
            DMA((ndev,)),
            DMA((ndev,)),
            DMA((CHUNKS * ndev,)),
            DMA((CHUNKS * ndev,)),
            DMA((CHUNKS * ndev,)),
            DMA((CHUNKS * ndev,)),
        ],
        compiler_params=pltpu.CompilerParams(
            collective_id=0, has_side_effects=True, vmem_limit_bytes=60 * 1024 * 1024
        ),
    )(
        frames.reshape(ndev, group, width),
        ref_rows,
        w_query,
        w_key,
        w_value,
        w_out,
        w_conv,
        t_query,
        t_key,
        t_value,
        t_out,
    )
    return out.reshape(fdev, pixels, width)


def solution(mesh):
    return jax.shard_map(
        per_device,
        mesh=mesh,
        in_specs=(
            P(("video", "frame"), None, None),
            P(("video", "frame"), None),
            P(),
            P(),
            P(),
            P(),
            P(),
            P(),
            P(),
            P(),
            P(),
        ),
        out_specs=P(("video", "frame"), None, None),
        check_vma=False,
    )
```
